512 devices in a mesh: resp: 8 (over z), fsdp: 16 (over y, core), head: 4 (over x).
Axes of the slice: x: 4, y: 8, z: 8, core: 2. Of those that a mesh axis runs over, the one named last changes fastest.
Arguments:
- queries: bfloat16 [32768, 4096], P(('resp', 'fsdp'), 'head'), may hold values from -12 to 12
- self_keys: bfloat16 [32768, 512], P(('resp', 'fsdp'), 'head'), may hold values from -12 to 12
- self_values: bfloat16 [32768, 512], P(('resp', 'fsdp'), 'head'), may hold values from -6 to 6
- d_out: bfloat16 [32768, 4096], P(('resp', 'fsdp'), 'head'), may hold values from -12 to 12
- prompt_keys: bfloat16 [16, 256, 512], P('resp', 'fsdp', 'head'), may hold values from -6 to 6
- prompt_values: bfloat16 [16, 256, 512], P('resp', 'fsdp', 'head'), may hold values from -6 to 6
- counts: int32 [16], replicated, may hold values from 1 to 16, 128 in all
- owner_slot: int32 [16], replicated, may hold values from 0 to 15, each once
- prompt_blocks: int32 [16], replicated, may hold values from 1 to 2
- resp_blocks: int32 [128], P(('resp', 'fsdp')), may hold values from 1 to 2
- grad_q: bfloat16 [8192, 4096], P('fsdp', ('resp', 'head')), may hold values from -4 to 4
- momentum: float32 [8192, 4096], P('fsdp', ('resp', 'head')), may hold values from -30 to 30
- basis: float32 [4096, 256], P(('resp', 'head')), may hold values from -0.09375 to 0.09375
Outputs:
- dq: bfloat16 [32768, 4096], P(('resp', 'fsdp'), 'head')
- resp_kv_grad: bfloat16 [2, 32768, 512], P(None, ('resp', 'fsdp'), 'head')
- prompt_kv_grad: float32 [2, 16, 256, 512], P(None, 'resp', 'fsdp', 'head')
- update: bfloat16 [8192, 4096], P('fsdp', ('resp', 'head'))
- momentum_out: float32 [8192, 4096], P('fsdp', ('resp', 'head'))
- basis_out: float32 [4096, 256], P(('resp', 'head'))
The draws below stay inside these ranges and needn't reach their ends.
Inputs may be any that keep to these rules, and one draw needn't show every extreme that they name: `counts`: responses are stored group by group in the order of the groups. `owner_slot`: each row of prompt_keys holds the prompt of exactly one group.
All inputs are finite; a program needn't handle non-finite values.
Results may differ from the reference program's by a relative error of at most 0.0087.
Values may be sent and summed in bfloat16 or wider, within the bound.
A program may use at most 64 MiB of HBM per device.

```python
import math
import jax
import jax.numpy as jnp
import numpy as np
from jax import lax

D = 8192
QH = 32
KVH = 4
HD = 128
QCOLS = 4096
RANK = 256
RLEN = 256
PLEN = 256
RESPONSES = 128
PROMPTS = 16
TOKENS = 32768


def drawn_pair(key):
    rows = RESPONSES * RLEN
    q_base = jnp.clip(jax.random.normal(jax.random.fold_in(key, 11), (rows, QH * HD), jnp.float32), -6.0, 6.0)
    k_base = jnp.clip(jax.random.normal(jax.random.fold_in(key, 12), (rows, KVH * HD), jnp.float32), -6.0, 6.0)
    return (q_base, k_base)


def draw_queries(key, part):
    return drawn_pair(key)[0].astype(jnp.bfloat16)


def draw_self_keys(key, part):
    return drawn_pair(key)[1].astype(jnp.bfloat16)


def draw_momentum(key, part):
    base = jnp.clip(jax.random.normal(jax.random.fold_in(key, 21), (D, QCOLS), jnp.float32), -5.0, 5.0)
    row_scale = jnp.exp(jax.random.uniform(jax.random.fold_in(key, 22), (D,), jnp.float32, 0.0, math.log(10.0)))
    rising = jnp.exp(math.log(3.0) * jnp.arange(D, dtype=jnp.float32) / D)
    col_scale = jnp.exp(jax.random.uniform(jax.random.fold_in(key, 23), (QCOLS,), jnp.float32, 0.0, math.log(10.0)))
    return 0.02 * base * (row_scale * rising)[:, None] * col_scale[None, :]


def tagged_blocks(key, number, largest, salt):
    values = jax.random.randint(jax.random.fold_in(key, salt), (number,), 1, largest + 1)
    marked = jax.random.randint(jax.random.fold_in(key, salt + 1), (), 0, number)
    return jnp.where(jnp.arange(number) == marked, largest, values).astype(jnp.int32)


def draw_prompt_blocks(key, part):
    return tagged_blocks(key, PROMPTS, PLEN // 128, 41)


def draw_resp_blocks(key, part):
    return tagged_blocks(key, RESPONSES, RLEN // 128, 51)


def steps_of(stream_key, shape, pieces, least, top_value):
    loudness = 1.0
    for axis_at, parts in pieces:
        heights = jax.random.uniform(jax.random.fold_in(jax.random.fold_in(stream_key, 6), axis_at), (parts,), jnp.float32, least / len(pieces), top_value / len(pieces))
        loudness = loudness * jnp.repeat(jnp.exp(heights), shape[axis_at] // parts).reshape((-1,) + (1,) * (len(shape) - 1 - axis_at))
    return loudness


def split_up(count, total, bound, skew):
    weights = [(1 << 20) // math.isqrt(grade ** skew) + 1 for grade in range(2, count + 1)]
    surplus, holding = total - bound - (count - 1), [1] * (count - 1)
    while surplus > 0:
        movable = [i for i in range(count - 1) if holding[i] < bound]
        whole, remaining = sum([weights[i] for i in movable]), surplus
        for i in movable:
            extra = min(bound - holding[i], max(1, remaining * weights[i] // whole), surplus)
            holding[i] = holding[i] + extra
            surplus = surplus - extra
    return np.array([bound] + holding)


def uneven(key, number_of, total, limit, slope):
    if number_of == 2:
        one = jax.random.randint(key, (), max(1, total - limit), min(limit, total - 1) + 1)
        return jnp.stack([one, total - one])
    sizes = jnp.asarray(split_up(number_of, total, limit, slope), jnp.int32)
    twos = (number_of - 1) // 2
    source_of, sink = sizes[1:1 + 2 * twos:2], sizes[2:2 + 2 * twos:2]
    margin = jnp.minimum(source_of - 1, limit - sink)
    passed = jax.random.randint(jax.random.fold_in(key, 1), (twos,), 0, 1 << 20) % (margin + 1)
    sizes = sizes.at[1:1 + 2 * twos:2].set(source_of - passed).at[2:2 + 2 * twos:2].set(sink + passed)
    return sizes[jax.random.permutation(jax.random.fold_in(key, 2), number_of)]


def bell_draw(stream_key, shape, scale, bound, shards=(), held_as=jnp.bfloat16):
    result = scale * jax.random.normal(stream_key, shape, jnp.float32)
    if shards:
        result = result * steps_of(stream_key, shape, shards, -0.22, 0.18)
    return jnp.clip(result, -bound, bound).astype(held_as)


def setup_inputs(seed: int = 0) -> dict:
    seeds = jax.random.split(jax.random.key(seed), 14)
    queries = draw_queries(jax.random.fold_in(seeds[13], 71), 0)
    self_keys = draw_self_keys(jax.random.fold_in(seeds[13], 71), 0)
    self_values = bell_draw(seeds[2], (TOKENS, KVH * HD), 1.0, 6.0, ((0, 128), (1, 4)))
    d_out = bell_draw(seeds[3], (TOKENS, QH * HD), 2.0, 12.0, ((0, 128), (1, 4)))
    prompt_keys = bell_draw(seeds[4], (PROMPTS, PLEN, KVH * HD), 1.0, 6.0, ((0, 8), (1, 16), (2, 4)))
    prompt_values = bell_draw(seeds[5], (PROMPTS, PLEN, KVH * HD), 1.0, 6.0, ((0, 8), (1, 16), (2, 4)))
    counts = uneven(seeds[6], PROMPTS, RESPONSES, 2 * RESPONSES // PROMPTS, 2).astype(jnp.int32)
    owner_slot = jax.random.permutation(seeds[7], PROMPTS).astype(jnp.int32)
    prompt_blocks = draw_prompt_blocks(jax.random.fold_in(seeds[13], 71), 0)
    resp_blocks = draw_resp_blocks(jax.random.fold_in(seeds[13], 71), 0)
    grad_q = bell_draw(seeds[10], (D, QCOLS), 0.3, 4.0, ((0, 16), (1, 32)))
    momentum = draw_momentum(jax.random.fold_in(seeds[13], 71), 0)
    basis = bell_draw(seeds[12], (QCOLS, RANK), QCOLS ** -0.5, 0.09375, ((0, 32),), jnp.float32)
    return dict(queries=queries, self_keys=self_keys, self_values=self_values, d_out=d_out, prompt_keys=prompt_keys, prompt_values=prompt_values, counts=counts, owner_slot=owner_slot, prompt_blocks=prompt_blocks, resp_blocks=resp_blocks, grad_q=grad_q, momentum=momentum, basis=basis)


def reference(queries, self_keys, self_values, d_out, prompt_keys, prompt_values, counts, owner_slot, prompt_blocks, resp_blocks, grad_q, momentum, basis):
    scale = HD ** (-0.5)
    per_group = QH // KVH
    width = PLEN + RLEN
    ends = jnp.cumsum(counts)
    order = jnp.arange(RESPONSES, dtype=jnp.int32)
    groups = lax.optimization_barrier(jnp.sum((ends[None, :] <= order[:, None]).astype(jnp.int32), axis=1))

    def one_response(accum, index):
        group = groups[index]
        stored = owner_slot[group]
        prompt_len = prompt_blocks[group] * 128
        resp_len = resp_blocks[index] * 128
        start = (index * RLEN).astype(jnp.int32)
        query = lax.dynamic_slice_in_dim(queries, start, RLEN, 0).astype(jnp.float32).reshape(RLEN, KVH, per_group, HD)
        keys = jnp.concatenate([prompt_keys[stored], lax.dynamic_slice_in_dim(self_keys, start, RLEN, 0)], 0)
        keys = keys.astype(jnp.float32).reshape(width, KVH, HD)
        values = jnp.concatenate([prompt_values[stored], lax.dynamic_slice_in_dim(self_values, start, RLEN, 0)], 0)
        values = values.astype(jnp.float32).reshape(width, KVH, HD)
        place = jnp.arange(width, dtype=jnp.int32)[None, :]
        position = jnp.arange(RLEN, dtype=jnp.int32)[:, None]
        inner = place - PLEN
        visible = jnp.where(place < PLEN, place < prompt_len, (inner <= position) & (inner < resp_len))
        logits = jnp.einsum('tngd,knd->ngtk', query, keys) * scale
        logits = jnp.where(visible, logits, -jnp.inf)
        peak = lax.optimization_barrier(jnp.max(logits, axis=3, keepdims=True))
        lse = peak + jnp.log(lax.optimization_barrier(jnp.sum(jnp.exp(logits - peak), axis=3, keepdims=True)))
        weight = lax.optimization_barrier(jnp.exp(logits - lse).astype(jnp.bfloat16)).astype(jnp.float32)
        output = jnp.einsum('ngtk,knd->tngd', weight, values)
        live = jnp.arange(RLEN, dtype=jnp.int32) < resp_len
        o_grad = jnp.where(live[:, None], lax.dynamic_slice_in_dim(d_out, start, RLEN, 0), 0)
        o_grad = o_grad.astype(jnp.float32).reshape(RLEN, KVH, per_group, HD)
        diag = lax.optimization_barrier(jnp.sum(o_grad * output, axis=3))
        p_grad = jnp.einsum('tngd,knd->ngtk', o_grad, values)
        s_grad = weight * (p_grad - jnp.transpose(diag, (1, 2, 0))[..., None])
        s_grad = lax.optimization_barrier(s_grad.astype(jnp.bfloat16)).astype(jnp.float32)
        q_grad = (jnp.einsum('ngtk,knd->tngd', s_grad, keys) * scale).reshape(RLEN, QH * HD).astype(jnp.bfloat16)
        k_grad = (jnp.einsum('ngtk,tngd->knd', s_grad, query) * scale).reshape(width, KVH * HD)
        v_grad = jnp.einsum('ngtk,tngd->knd', weight, o_grad).reshape(width, KVH * HD)
        accum = accum.at[:, stored].add(jnp.stack([k_grad[:PLEN], v_grad[:PLEN]], 0))
        own = jnp.stack([k_grad[PLEN:], v_grad[PLEN:]], 0).astype(jnp.bfloat16)
        return (accum, (q_grad, own))
    start_accum = jnp.zeros((2, PROMPTS, PLEN, KVH * HD), jnp.float32)
    prompt_grad, (q_grads, own_grads) = lax.scan(one_response, start_accum, order)
    dq = q_grads.reshape(TOKENS, QH * HD)
    resp_grad = jnp.transpose(own_grads, (1, 0, 2, 3)).reshape(2, TOKENS, KVH * HD)
    highest = lax.Precision.HIGHEST
    total = momentum + grad_q.astype(jnp.float32)
    projected = jnp.dot(total, basis, precision=highest)
    gram = jnp.dot(projected.T, projected, precision=highest)
    lower = jnp.linalg.cholesky(gram)
    ortho = jax.scipy.linalg.solve_triangular(lower, projected.T, lower=True).T
    back = jnp.dot(total.T, ortho, precision=highest)
    momentum_out = total - 0.05 * jnp.dot(ortho, back.T, precision=highest)
    basis_out = back * lax.rsqrt(lax.optimization_barrier(jnp.sum(back * back, axis=0)) + 1e-06)
    update = (math.sqrt(D * QCOLS / RANK) * jnp.dot(ortho, basis_out.T, precision=highest)).astype(jnp.bfloat16)
    return (dq, resp_grad, prompt_grad, update, momentum_out, basis_out)
```

```python
import math

import jax
import jax.numpy as jnp
from jax import lax
from jax.experimental import pallas as pl
from jax.experimental.pallas import tpu as pltpu
from jax.sharding import PartitionSpec as P

MESH = pl.DeviceIdType.MESH
HIGHEST = lax.Precision.HIGHEST
F32 = jnp.float32
BF16 = jnp.bfloat16

NR, NF, NH = 8, 16, 4
HD = 128
RANK = 256
GAIN = math.sqrt(8192 * 4096 / 256)
COPIES = 103


def mm(a, b, ca, cb, precision=None):
    return lax.dot_general(
        a, b, (((ca,), (cb,)), ((), ())), precision=precision, preferred_element_type=F32
    )


def exact(a, b, ca, cb):
    return mm(a, b, ca, cb, HIGHEST)


class Net:
    def __init__(self, sent, arrived):
        self.sent, self.arrived, self.n = sent, arrived, 0
        self.open = []

    def copy(self, src, dst, lands, device):
        at = self.n
        self.n += 1
        go = pltpu.make_async_remote_copy(
            src_ref=src, dst_ref=dst, send_sem=self.sent.at[at], recv_sem=self.arrived.at[at],
            device_id=device, device_id_type=MESH,
        )
        come = pltpu.make_async_remote_copy(
            src_ref=src, dst_ref=lands, send_sem=self.sent.at[at], recv_sem=self.arrived.at[at],
            device_id=device, device_id_type=MESH,
        )
        go.start()
        self.open.append(go)
        return come

    def finish(self):
        for c in self.open:
            c.wait_send()


def whole_factor(a_ref, x_ref, o_ref):
    row = lax.broadcasted_iota(jnp.int32, (8, 128), 0)
    r128 = lax.broadcasted_iota(jnp.int32, (128, 128), 0)
    c128 = lax.broadcasted_iota(jnp.int32, (128, 128), 1)
    x_ref[...] = jnp.where(r128 == c128, 1.0, 0.0).astype(F32)

    def line(v, j):
        return jnp.broadcast_to(v[j : j + 1, :], (8, 128))

    def lane(v, j):
        return jnp.broadcast_to(v[:, j : j + 1], (8, 128))

    def panel(p, carry):
        at = pl.ds(pl.multiple_of(p * 8, 8), 8)
        turn = lax.rem(128 - p * 8, 128)
        z, zx = a_ref[at, :], x_ref[at, :]
        turned = pltpu.roll(z, turn, 1)
        cols = [lane(turned, j) for j in range(8)]
        out = jnp.zeros((8, 128), F32)
        for j in range(8):
            pivot = line(cols[j], j)
            inv = 1.0 / pivot
            root = lax.rsqrt(pivot)
            root = root * (1.5 - 0.5 * pivot * root * root)
            coef = cols[j] * inv
            here = row == j
            zj, zxj = line(z, j), line(zx, j)
            out = jnp.where(here, zxj * root, out)
            z = jnp.where(here, zj * inv, z - coef * zj)
            zx = jnp.where(here, zxj * inv, zx - coef * zxj)
            for m in range(j + 1, 8):
                cm = line(cols[m], j)
                cols[m] = jnp.where(here, cm * inv, cols[m] - coef * cm)
        o_ref[at, :] = out
        zs = [line(z, j) for j in range(8)]
        zxs = [line(zx, j) for j in range(8)]
        for t in range(1, 16):
            below = jnp.where(p < t, 1.0, 0.0).astype(F32)
            a_t, x_t = a_ref[8 * t : 8 * t + 8, :], x_ref[8 * t : 8 * t + 8, :]
            turned = pltpu.roll(a_t, turn, 1) * below
            for j in range(8):
                c = lane(turned, j)
                a_t = a_t - c * zs[j]
                x_t = x_t - c * zxs[j]
            a_ref[8 * t : 8 * t + 8, :] = a_t
            x_ref[8 * t : 8 * t + 8, :] = x_t
        return carry

    lax.fori_loop(0, 16, panel, 0)


def kernel(
    q_ref, sk_ref, sv_ref, do_ref, pk_ref, pv_ref, counts_ref, owner_ref, pblk_ref, rblk_ref,
    gq_ref, mom_ref, basis_ref,
    dq_ref, kv_ref, pg_ref, upd_ref, mo_ref, bo_ref,
    total, pp, xr, xs, s1, zr, pf, gy, fr, gs, yr, gyf, evk, evv, sel, kvb, bias, gm, kt, acc,
    ret, ret_in, bys, bys_in, sqx, sqz, fa, fx, li, orth, back, sent, arrived,
):
    r, f, h = lax.axis_index("resp"), lax.axis_index("fsdp"), lax.axis_index("head")
    y, c = f // 2, f % 2
    net = Net(sent, arrived)
    right, left = (h + 1) % NH, (h + 3) % NH
    scale = HD ** -0.5

    def zpeer(d):
        return (r + d) % NR

    def fpeer(d):
        return (f + d) % NF

    def ypeer(d):
        return (y + d) % 8

    barrier = pltpu.get_barrier_semaphore()
    for d in range(1, NH):
        pl.semaphore_signal(barrier, inc=1, device_id=(r, f, (h + d) % NH), device_id_type=MESH)
    for d in range(1, NR):
        pl.semaphore_signal(barrier, inc=1, device_id=(zpeer(d), f, h), device_id_type=MESH)
    for d in range(1, NF):
        pl.semaphore_signal(barrier, inc=1, device_id=(r, fpeer(d), h), device_id_type=MESH)

    total[...] = mom_ref[...] + gq_ref[...].astype(F32)
    for k in range(8):
        pp[k] = exact(total[64 * k : 64 * k + 64, :], basis_ref[...], 1, 0)
    evk[r] = pk_ref[...]
    evv[r] = pv_ref[...]

    ends = []
    run = jnp.int32(0)
    for g in range(16):
        run = run + counts_ref[g]
        ends.append(run)

    def group_of(order):
        n = jnp.int32(0)
        for g in range(15):
            n = n + jnp.where(ends[g] <= order, 1, 0).astype(jnp.int32)
        return n

    slots = [owner_ref[group_of(r * NF + k)] for k in range(NF)]
    plen = pblk_ref[group_of(r * NF + f)] * 128
    rlen = rblk_ref[0] * 128

    pl.semaphore_wait(barrier, (NH - 1) + (NR - 1) + (NF - 1))

    opp = (h + 2) % NH
    to_r, to_l = (r, f, right), (r, f, left)
    rel_l = net.copy(pp.at[opp * 2], xr.at[0], xr.at[0], to_r)
    rel_r = net.copy(pp.at[opp * 2 + 1], xr.at[1], xr.at[1], to_l)
    ev_in = []
    for d in range(1, NR):
        src = (r + NR - d) % NR
        ev_in.append(net.copy(pk_ref, evk.at[r], evk.at[src], (zpeer(d), f, h)))
        ev_in.append(net.copy(pv_ref, evv.at[r], evv.at[src], (zpeer(d), f, h)))
    dir_l = net.copy(pp.at[right * 2 + 1], xr.at[2], xr.at[2], to_r)
    dir_r = net.copy(pp.at[left * 2], xr.at[3], xr.at[3], to_l)

    key = lax.broadcasted_iota(jnp.int32, (512, 256), 0)
    tok = lax.broadcasted_iota(jnp.int32, (512, 256), 1)
    inner = key - 256
    seen = ((key < 256) & (key < plen)) | ((key >= 256) & (inner <= tok) & (inner < rlen))
    bias[...] = jnp.where(seen, 0.0, -jnp.inf).astype(F32)
    live = lax.broadcasted_iota(jnp.int32, (256, 1024), 0) < rlen
    gm[...] = jnp.where(live, do_ref[...].astype(F32), 0.0).astype(BF16)
    kvb[0, 16:32] = sk_ref[...].reshape(16, 16, 128)
    kvb[1, 16:32] = sv_ref[...].reshape(16, 16, 128)
    acc[...] = jnp.zeros_like(acc)

    rel_l.wait_recv()
    xs[0] = xr[0] + pp[right * 2]
    com_l = net.copy(xs.at[0], xr.at[4], xr.at[4], to_r)
    rel_r.wait_recv()
    xs[1] = xr[1] + pp[left * 2 + 1]
    com_r = net.copy(xs.at[1], xr.at[5], xr.at[5], to_l)

    for m in ev_in:
        m.wait_recv()
    for k in range(NF):
        s = slots[k]
        sel[k, 0] = evk[s // 2, s % 2]
        sel[k, 1] = evv[s // 2, s % 2]
    kv_in = []
    for d in range(1, NF):
        src = (f + NF - d) % NF
        kv_in.append(net.copy(sel.at[fpeer(d)], kvb.at[:, f], kvb.at[:, src], (r, fpeer(d), h)))
    kvb[:, f] = sel[f]

    dir_r.wait_recv()
    com_l.wait_recv()
    half_a = pp[h * 2] + (xr[3] + xr[4])
    s1[0:4] = half_a.reshape(4, 16, 256)
    dir_l.wait_recv()
    com_r.wait_recv()
    half_b = pp[h * 2 + 1] + (xr[2] + xr[5])
    s1[4:8] = half_b.reshape(4, 16, 256)

    z_in = [
        net.copy(s1.at[zpeer(d)], zr.at[d], zr.at[d], (zpeer(d), f, h)) for d in range(1, NR)
    ]

    for m in kv_in:
        m.wait_recv()
    keys = kvb[0].reshape(512, 128)
    kt[...] = keys.astype(F32).T.astype(BF16)

    def head_step(k, carry):
        cols = pl.ds(pl.multiple_of(k * HD, HD), HD)
        q, g = q_ref[:, cols], gm[:, cols]
        s = mm(kvb[0].reshape(512, 128), q, 1, 1) * scale + bias[...]
        e = jnp.exp(s - jnp.max(s, axis=0, keepdims=True))
        p = (e * (1.0 / jnp.sum(e, axis=0, keepdims=True))).astype(BF16)
        dp = mm(kvb[1].reshape(512, 128), g, 1, 1)
        pw = p.astype(F32)
        ds = (pw * (dp - jnp.sum(pw * dp, axis=0, keepdims=True))).astype(BF16)
        dq_ref[:, cols] = (mm(kt[...], ds, 1, 0) * scale).T.astype(BF16)
        acc[0] += mm(ds, q, 1, 0)
        acc[1] += mm(p, g, 1, 0)
        return carry

    lax.fori_loop(0, 2, head_step, 0)

    for m in z_in:
        m.wait_recv()
    mine = s1[r]
    for d in range(1, NR):
        mine = mine + zr[d]
    spot = pl.ds(pl.multiple_of((r % 4) * 16, 16), 16)
    pf[h * 2 + r // 4, spot, :] = mine
    g_in = []
    for d in range(1, NR):
        src = (r + NR - d) % NR
        s_spot = pl.ds(pl.multiple_of((src % 4) * 16, 16), 16)
        here = pf.at[h * 2 + r // 4, spot]
        g_in.append(net.copy(here, here, pf.at[h * 2 + src // 4, s_spot], (zpeer(d), f, h)))

    lax.fori_loop(2, 4, head_step, 0)

    for m in g_in:
        m.wait_recv()
    def half(q, b):
        return pf.at[q * 2 + b]

    la = net.copy(half(h, 0), half(h, 0), half(left, 0), to_r)
    rb = net.copy(half(h, 1), half(h, 1), half(right, 1), to_l)
    lb = net.copy(half(h, 1), half(h, 1), half(left, 1), to_r)
    ra = net.copy(half(h, 0), half(h, 0), half(right, 0), to_l)

    lax.fori_loop(4, 5, head_step, 0)

    la.wait_recv()
    oa = net.copy(half(left, 0), half(left, 0), half(opp, 0), to_r)
    rb.wait_recv()
    ob = net.copy(half(right, 1), half(right, 1), half(opp, 1), to_l)

    lax.fori_loop(5, 6, head_step, 0)

    for m in (lb, ra, oa, ob):
        m.wait_recv()
    proj = pf[...].reshape(512, 256)
    gram = exact(proj, proj, 0, 0)
    cross = exact(total[...], proj, 0, 0)
    gy[0] = gram[0:192]
    gy[1, 0:64] = gram[192:256]
    gy[1, 64:192] = cross

    mate = (r, f + 1 - 2 * c, h)
    first = net.copy(gy.at[1 - c], fr, fr, mate)
    lax.fori_loop(6, 7, head_step, 0)
    first.wait_recv()
    gs[...] = (gy[c] + fr[...]).reshape(8, 24, 256)
    y_in = [
        net.copy(gs.at[ypeer(d)], yr.at[d], yr.at[d], (r, ypeer(d) * 2 + c, h))
        for d in range(1, 8)
    ]
    lax.fori_loop(7, 8, head_step, 0)

    k_all, v_all = acc[0] * scale, acc[1]
    kv_ref[0] = k_all[256:512].astype(BF16)
    kv_ref[1] = v_all[256:512].astype(BF16)
    ret[:, 0] = k_all[0:256].reshape(16, 16, 128)
    ret[:, 1] = v_all[0:256].reshape(16, 16, 128)

    for m in y_in:
        m.wait_recv()
    piece = gs[y]
    for d in range(1, 8):
        piece = piece + yr[d]
    gyf[c, y] = piece
    yg_in = []
    for d in range(1, 8):
        src = (y + 8 - d) % 8
        yg_in.append(
            net.copy(gyf.at[c, y], gyf.at[c, y], gyf.at[c, src], (r, ypeer(d) * 2 + c, h))
        )
    ret_arr = [
        net.copy(ret.at[fpeer(d)], ret_in.at[d], ret_in.at[d], (r, fpeer(d), h))
        for d in range(1, NF)
    ]
    for m in yg_in:
        m.wait_recv()
    last = net.copy(gyf.at[c], gyf.at[c], gyf.at[1 - c], mate)
    last.wait_recv()

    low = gyf[0].reshape(192, 256)
    high = gyf[1].reshape(192, 256)
    fa[...] = low[0:128, 0:128]
    g21 = jnp.concatenate([low[128:192, 0:128], high[0:64, 0:128]], 0)
    g22 = jnp.concatenate([low[128:192, 128:256], high[0:64, 128:256]], 0)
    whole_factor(fa, fx, li.at[0])
    i11 = li[0]
    l21 = exact(g21, i11, 1, 1)
    fa[...] = g22 - exact(l21, l21, 1, 1)
    li[2] = exact(l21, i11, 1, 0)

    for m in ret_arr:
        m.wait_recv()
    ret_in[0] = ret[f]
    for s in range(16):
        tot = jnp.zeros((2, 16, 128), F32)
        for d in range(NF):
            tot = tot + jnp.where(slot_at(slots, f, d) == s, ret_in[d], 0.0)
        bys[s // 2, :, s % 2] = tot
    b_in = [
        net.copy(bys.at[zpeer(d)], bys_in.at[d], bys_in.at[d], (zpeer(d), f, h))
        for d in range(1, NR)
    ]

    whole_factor(fa, fx, li.at[1])
    i22 = li[1]
    i21 = -exact(i22, li[2], 1, 0)

    def times_inverse(m):
        first_part = exact(m[:, 0:128], i11, 1, 1)
        second = exact(m[:, 0:128], i21, 1, 1) + exact(m[:, 128:256], i22, 1, 1)
        return first_part, second

    b1, b2 = times_inverse(gyf[1].reshape(192, 256)[64:192])
    back[:, 0:128] = b1
    back[:, 128:256] = b2
    bk = back[...]
    sq = jnp.sum(bk * bk, axis=0, keepdims=True)
    sqx[0] = sq
    x_in = [
        net.copy(sqx.at[0], sqx.at[d], sqx.at[d], (r, f, (h + d) % NH)) for d in range(1, NH)
    ]
    o1, o2 = times_inverse(pf[...].reshape(512, 256))
    orth[:, 0:128] = o1
    orth[:, 128:256] = o2
    for m in x_in:
        m.wait_recv()
    sqz[0] = (sqx[0] + sqx[2]) + (sqx[1] + sqx[3])
    q_in = [
        net.copy(sqz.at[0], sqz.at[d], sqz.at[d], (zpeer(d), f, h)) for d in range(1, NR)
    ]
    mo_ref[...] = total[...] - 0.05 * exact(orth[...], bk, 1, 1)
    for m in b_in:
        m.wait_recv()
    owned = bys[r]
    for d in range(1, NR):
        owned = owned + bys_in[d]
    pg_ref[...] = owned
    for m in q_in:
        m.wait_recv()
    squares = sqz[0]
    for d in range(1, NR):
        squares = squares + sqz[d]
    new = bk * lax.rsqrt(squares + 1e-06)
    bo_ref[...] = new
    upd_ref[...] = (GAIN * exact(orth[...], new, 1, 1)).astype(BF16)
    net.finish()


def slot_at(slots, f, d):
    at = (f + NF - d) % NF
    found = slots[0]
    for k in range(1, NF):
        found = jnp.where(at == k, slots[k], found)
    return found


def on_device(*args):
    vm = pl.BlockSpec(memory_space=pltpu.VMEM)
    sm = pl.BlockSpec(memory_space=pltpu.SMEM)
    v = pltpu.VMEM
    return pl.pallas_call(
        kernel,
        out_shape=(
            jax.ShapeDtypeStruct((256, 1024), BF16),
            jax.ShapeDtypeStruct((2, 256, 128), BF16),
            jax.ShapeDtypeStruct((2, 2, 16, 128), F32),
            jax.ShapeDtypeStruct((512, 128), BF16),
            jax.ShapeDtypeStruct((512, 128), F32),
            jax.ShapeDtypeStruct((128, 256), F32),
        ),
        in_specs=[vm] * 6 + [sm] * 4 + [vm] * 3,
        out_specs=(vm,) * 6,
        scratch_shapes=[
            v((512, 128), F32),
            v((8, 64, 256), F32),
            v((6, 64, 256), F32),
            v((2, 64, 256), F32),
            v((8, 16, 256), F32),
            v((8, 16, 256), F32),
            v((8, 64, 256), F32),
            v((2, 192, 256), F32),
            v((192, 256), F32),
            v((8, 24, 256), F32),
            v((8, 24, 256), F32),
            v((2, 8, 24, 256), F32),
            v((8, 2, 16, 128), BF16),
            v((8, 2, 16, 128), BF16),
            v((16, 2, 16, 128), BF16),
            v((2, 32, 16, 128), BF16),
            v((512, 256), F32),
            v((256, 1024), BF16),
            v((128, 512), BF16),
            v((2, 512, 128), F32),
            v((16, 2, 16, 128), F32),
            v((16, 2, 16, 128), F32),
            v((8, 2, 2, 16, 128), F32),
            v((8, 2, 2, 16, 128), F32),
            v((4, 1, 256), F32),
            v((8, 1, 256), F32),
            v((128, 128), F32),
            v((128, 128), F32),
            v((3, 128, 128), F32),
            v((512, 256), F32),
            v((128, 256), F32),
            pltpu.SemaphoreType.DMA((COPIES,)),
            pltpu.SemaphoreType.DMA((COPIES,)),
        ],
        compiler_params=pltpu.CompilerParams(collective_id=0, has_side_effects=True),
    )(*args)


def solution(mesh):
    placed = (
        P(("resp", "fsdp"), "head"),
        P(("resp", "fsdp"), "head"),
        P(("resp", "fsdp"), "head"),
        P(("resp", "fsdp"), "head"),
        P("resp", "fsdp", "head"),
        P("resp", "fsdp", "head"),
        P(),
        P(),
        P(),
        P(("resp", "fsdp")),
        P("fsdp", ("resp", "head")),
        P("fsdp", ("resp", "head")),
        P(("resp", "head"), None),
    )
    return jax.shard_map(
        on_device,
        mesh=mesh,
        in_specs=placed,
        out_specs=(
            P(("resp", "fsdp"), "head"),
            P(None, ("resp", "fsdp"), "head"),
            P(None, "resp", "fsdp", "head"),
            P("fsdp", ("resp", "head")),
            P("fsdp", ("resp", "head")),
            P(("resp", "head"), None),
        ),
        check_vma=False,
    )
```

```python
import math

import jax
import jax.numpy as jnp
from jax import lax
from jax.experimental import pallas as pl
from jax.experimental.pallas import tpu as pltpu
from jax.sharding import PartitionSpec as P

MESH = pl.DeviceIdType.MESH
HIGHEST = lax.Precision.HIGHEST
F32 = jnp.float32
BF16 = jnp.bfloat16

NR, NF, NH = 8, 16, 4
HD = 128
RANK = 256
GAIN = math.sqrt(8192 * 4096 / 256)
COPIES = 126


def mm(a, b, ca, cb, precision=None):
    return lax.dot_general(
        a, b, (((ca,), (cb,)), ((), ())), precision=precision, preferred_element_type=F32
    )


def exact(a, b, ca, cb):
    return mm(a, b, ca, cb, HIGHEST)


class Net:
    def __init__(self, sent, arrived):
        self.sent, self.arrived, self.n = sent, arrived, 0
        self.open = []

    def copy(self, src, dst, lands, device):
        at = self.n
        self.n += 1
        go = pltpu.make_async_remote_copy(
            src_ref=src, dst_ref=dst, send_sem=self.sent.at[at], recv_sem=self.arrived.at[at],
            device_id=device, device_id_type=MESH,
        )
        come = pltpu.make_async_remote_copy(
            src_ref=src, dst_ref=lands, send_sem=self.sent.at[at], recv_sem=self.arrived.at[at],
            device_id=device, device_id_type=MESH,
        )
        go.start()
        self.open.append(go)
        return come

    def finish(self):
        for c in self.open:
            c.wait_send()


def whole_factor(a_ref, x_ref, o_ref):
    row = lax.broadcasted_iota(jnp.int32, (8, 128), 0)
    r128 = lax.broadcasted_iota(jnp.int32, (128, 128), 0)
    c128 = lax.broadcasted_iota(jnp.int32, (128, 128), 1)
    x_ref[...] = jnp.where(r128 == c128, 1.0, 0.0).astype(F32)

    def line(v, j):
        return jnp.broadcast_to(v[j : j + 1, :], (8, 128))

    def lanes(v, start):
        return [
            jnp.take_along_axis(v, jnp.full((8, 128), start + j, jnp.int32), axis=1)
            for j in range(8)
        ]

    def reciprocal(v):
        guess = pl.reciprocal(v, approx=True)
        guess = guess * (2.0 - v * guess)
        return guess * (2.0 - v * guess)

    def root(v):
        guess = lax.rsqrt(v)
        return guess * (1.5 - 0.5 * v * guess * guess)

    def reduce_panel(z, zx, start):
        cols = lanes(z, start)
        out = jnp.zeros((8, 128), F32)
        for j in range(0, 8, 2):
            one, two = row == j, row == j + 1
            pair = one | two
            a, b, d = line(cols[j], j), line(cols[j + 1], j), line(cols[j + 1], j + 1)
            det = a * d - b * b
            inv = reciprocal(det)
            i11, i12, i22 = d * inv, -(b * inv), a * inv
            f1 = jnp.where(one, -i11, jnp.where(two, -i12, cols[j] * i11 + cols[j + 1] * i12))
            f2 = jnp.where(one, -i12, jnp.where(two, -i22, cols[j] * i12 + cols[j + 1] * i22))

            def sweep(v):
                return jnp.where(pair, 0.0, v) - (f1 * line(v, j) + f2 * line(v, j + 1))

            first, second = line(zx, j), line(zx, j + 1)
            up = reciprocal(a)
            out = jnp.where(one, first * root(a), out)
            out = jnp.where(two, (second - (b * up) * first) * root(det * up), out)
            for m in range(j + 2, 8):
                cols[m] = sweep(cols[m])
            z, zx = sweep(z), sweep(zx)
        return z, zx, out

    def take(v, c, lines):
        t = [c[j] * lines[j] for j in range(8)]
        return v - (((t[0] + t[1]) + (t[2] + t[3])) + ((t[4] + t[5]) + (t[6] + t[7])))

    z, zx, out = reduce_panel(a_ref[0:8, :], x_ref[0:8, :], 0)
    o_ref[0:8, :] = out

    def step(p, carry):
        z, zx = carry
        zs, zxs = [line(z, j) for j in range(8)], [line(zx, j) for j in range(8)]
        at = pl.ds(pl.multiple_of(p * 8 + 8, 8), 8)
        nz = a_ref[at, :]
        c = lanes(nz, p * 8)
        nz, nzx = take(nz, c, zs), take(x_ref[at, :], c, zxs)
        nz, nzx, out = reduce_panel(nz, nzx, p * 8 + 8)
        for t in range(2, 16):
            below = jnp.where(p + 1 < t, 1.0, 0.0).astype(F32)
            here = slice(8 * t, 8 * t + 8)
            a_t = a_ref[here, :]
            c = lanes(a_t * below, p * 8)
            a_ref[here, :] = take(a_t, c, zs)
            x_ref[here, :] = take(x_ref[here, :], c, zxs)
        o_ref[at, :] = out
        return nz, nzx

    lax.fori_loop(0, 15, step, (z, zx))


def kernel(
    q_hbm, sk_hbm, sv_hbm, do_hbm, pk_hbm, pv_hbm, counts_hbm, owner_hbm, pblk_hbm, rblk_ref,
    gq_hbm, mom_hbm, basis_hbm,
    dq_ref, kv_ref, pg_ref, upd_ref, mo_ref, bo_ref,
    q_ref, sk_ref, sv_ref, do_ref, pk_ref, pv_ref, counts_ref, owner_ref, pblk_ref,
    gq_ref, mom_ref, basis_ref, total, pp, xr, xs, s1, zr, pf, gy, fr, gs, yr, gyf, cy, cfr, cgs, cyr, cyf, evk, evv, sel, kvb, bias, gm, kt, acc,
    ret, ret_in, bys, bys_in, sqx, sqz, fa, fx, li, orth, back, loaded, sent, arrived,
):
    r, f, h = lax.axis_index("resp"), lax.axis_index("fsdp"), lax.axis_index("head")
    y, c = f // 2, f % 2
    net = Net(sent, arrived)
    right, left = (h + 1) % NH, (h + 3) % NH
    scale = HD ** -0.5

    def zpeer(d):
        return (r + d) % NR

    def fpeer(d):
        return (f + d) % NF

    def ypeer(d):
        return (y + d) % 8

    barrier = pltpu.get_barrier_semaphore()
    for d in range(1, NH):
        pl.semaphore_signal(barrier, inc=1, device_id=(r, f, (h + d) % NH), device_id_type=MESH)
    for d in range(1, NR):
        pl.semaphore_signal(barrier, inc=1, device_id=(zpeer(d), f, h), device_id_type=MESH)
    for d in range(1, NF):
        pl.semaphore_signal(barrier, inc=1, device_id=(r, fpeer(d), h), device_id_type=MESH)

    def load(k, src, dst):
        c = pltpu.make_async_copy(src, dst, loaded.at[k])
        c.start()
        return c

    mains = [
        load(0, mom_hbm, mom_ref), load(1, gq_hbm, gq_ref), load(2, basis_hbm, basis_ref),
    ]
    prompts = [
        load(3, pk_hbm, pk_ref), load(4, pv_hbm, pv_ref), load(5, counts_hbm, counts_ref),
        load(6, owner_hbm, owner_ref), load(7, pblk_hbm, pblk_ref),
    ]
    others = [
        load(8, do_hbm, do_ref), load(9, sk_hbm, sk_ref), load(10, sv_hbm, sv_ref),
        load(11, q_hbm, q_ref),
    ]

    for m in mains:
        m.wait()
    total[...] = mom_ref[...] + gq_ref[...].astype(F32)
    for k in range(8):
        pp[k] = exact(total[64 * k : 64 * k + 64, :], basis_ref[...], 1, 0)
    for m in prompts:
        m.wait()
    evk[r] = pk_ref[...]
    evv[r] = pv_ref[...]

    ends = []
    run = jnp.int32(0)
    for g in range(16):
        run = run + counts_ref[g]
        ends.append(run)

    def group_of(order):
        n = jnp.int32(0)
        for g in range(15):
            n = n + jnp.where(ends[g] <= order, 1, 0).astype(jnp.int32)
        return n

    slots = [owner_ref[group_of(r * NF + k)] for k in range(NF)]
    plen = pblk_ref[group_of(r * NF + f)] * 128
    rlen = rblk_ref[0] * 128

    pl.semaphore_wait(barrier, (NH - 1) + (NR - 1) + (NF - 1))

    opp = (h + 2) % NH
    to_r, to_l = (r, f, right), (r, f, left)
    rel_l = net.copy(pp.at[opp * 2], xr.at[0], xr.at[0], to_r)
    rel_r = net.copy(pp.at[opp * 2 + 1], xr.at[1], xr.at[1], to_l)
    ev_in = []
    for d in range(1, NR):
        src = (r + NR - d) % NR
        ev_in.append(net.copy(pk_ref, evk.at[r], evk.at[src], (zpeer(d), f, h)))
        ev_in.append(net.copy(pv_ref, evv.at[r], evv.at[src], (zpeer(d), f, h)))
    dir_l = net.copy(pp.at[right * 2 + 1], xr.at[2], xr.at[2], to_r)
    dir_r = net.copy(pp.at[left * 2], xr.at[3], xr.at[3], to_l)

    for m in others:
        m.wait()
    key = lax.broadcasted_iota(jnp.int32, (512, 256), 0)
    tok = lax.broadcasted_iota(jnp.int32, (512, 256), 1)
    inner = key - 256
    seen = ((key < 256) & (key < plen)) | ((key >= 256) & (inner <= tok) & (inner < rlen))
    bias[...] = jnp.where(seen, 0.0, -jnp.inf).astype(F32)
    live = lax.broadcasted_iota(jnp.int32, (256, 1024), 0) < rlen
    gm[...] = jnp.where(live, do_ref[...].astype(F32), 0.0).astype(BF16)
    kvb[0, 16:32] = sk_ref[...].reshape(16, 16, 128)
    kvb[1, 16:32] = sv_ref[...].reshape(16, 16, 128)
    acc[...] = jnp.zeros_like(acc)

    rel_l.wait_recv()
    xs[0] = xr[0] + pp[right * 2]
    com_l = net.copy(xs.at[0], xr.at[4], xr.at[4], to_r)
    rel_r.wait_recv()
    xs[1] = xr[1] + pp[left * 2 + 1]
    com_r = net.copy(xs.at[1], xr.at[5], xr.at[5], to_l)

    for m in ev_in:
        m.wait_recv()
    for k in range(NF):
        s = slots[k]
        sel[k, 0] = evk[s // 2, s % 2]
        sel[k, 1] = evv[s // 2, s % 2]
    kv_in = []
    for d in range(1, NF):
        src = (f + NF - d) % NF
        kv_in.append(net.copy(sel.at[fpeer(d)], kvb.at[:, f], kvb.at[:, src], (r, fpeer(d), h)))
    kvb[:, f] = sel[f]

    dir_r.wait_recv()
    com_l.wait_recv()
    half_a = pp[h * 2] + (xr[3] + xr[4])
    s1[0:4] = half_a.reshape(4, 16, 256)
    dir_l.wait_recv()
    com_r.wait_recv()
    half_b = pp[h * 2 + 1] + (xr[2] + xr[5])
    s1[4:8] = half_b.reshape(4, 16, 256)

    z_in = [
        net.copy(s1.at[zpeer(d)], zr.at[d], zr.at[d], (zpeer(d), f, h)) for d in range(1, NR)
    ]

    for m in kv_in:
        m.wait_recv()
    keys = kvb[0].reshape(512, 128)
    kt[...] = keys.astype(F32).T.astype(BF16)

    def head_step(k, carry):
        cols = pl.ds(pl.multiple_of(k * HD, HD), HD)
        q, g = q_ref[:, cols], gm[:, cols]
        s = mm(kvb[0].reshape(512, 128), q, 1, 1) * scale + bias[...]
        e = jnp.exp(s - jnp.max(s, axis=0, keepdims=True))
        p = (e * (1.0 / jnp.sum(e, axis=0, keepdims=True))).astype(BF16)
        dp = mm(kvb[1].reshape(512, 128), g, 1, 1)
        pw = p.astype(F32)
        ds = (pw * (dp - jnp.sum(pw * dp, axis=0, keepdims=True))).astype(BF16)
        dq_ref[:, cols] = (mm(kt[...], ds, 1, 0) * scale).T.astype(BF16)
        acc[0] += mm(ds, q, 1, 0)
        acc[1] += mm(p, g, 1, 0)
        return carry

    lax.fori_loop(0, 2, head_step, 0)

    for m in z_in:
        m.wait_recv()
    mine = s1[r]
    for d in range(1, NR):
        mine = mine + zr[d]
    spot = pl.ds(pl.multiple_of((r % 4) * 16, 16), 16)
    pf[h * 2 + r // 4, spot, :] = mine
    g_in = []
    for d in range(1, NR):
        src = (r + NR - d) % NR
        s_spot = pl.ds(pl.multiple_of((src % 4) * 16, 16), 16)
        here = pf.at[h * 2 + r // 4, spot]
        g_in.append(net.copy(here, here, pf.at[h * 2 + src // 4, s_spot], (zpeer(d), f, h)))

    lax.fori_loop(2, 4, head_step, 0)

    for m in g_in:
        m.wait_recv()
    def half(q, b):
        return pf.at[q * 2 + b]

    la = net.copy(half(h, 0), half(h, 0), half(left, 0), to_r)
    rb = net.copy(half(h, 1), half(h, 1), half(right, 1), to_l)
    lb = net.copy(half(h, 1), half(h, 1), half(left, 1), to_r)
    ra = net.copy(half(h, 0), half(h, 0), half(right, 0), to_l)

    lax.fori_loop(4, 5, head_step, 0)

    la.wait_recv()
    oa = net.copy(half(left, 0), half(left, 0), half(opp, 0), to_r)
    rb.wait_recv()
    ob = net.copy(half(right, 1), half(right, 1), half(opp, 1), to_l)

    lax.fori_loop(5, 6, head_step, 0)

    for m in (lb, ra, oa, ob):
        m.wait_recv()
    proj = pf[...].reshape(512, 256)
    p1, p2 = proj[:, 0:128], proj[:, 128:256]
    g11, g21, g22 = exact(p1, p1, 0, 0), exact(p2, p1, 0, 0), exact(p2, p2, 0, 0)
    gy[0, 0:128], gy[0, 128:192] = g11, g21[0:64]
    gy[1, 0:64], gy[1, 64:192] = g21[64:128], g22

    mate = (r, f + 1 - 2 * c, h)
    first = net.copy(gy.at[1 - c], fr, fr, mate)
    cross = exact(total[...], proj, 0, 0)
    cy[0], cy[1] = cross[0:64], cross[64:128]
    first.wait_recv()
    gs[...] = (gy[c] + fr[...]).reshape(8, 24, 128)
    y_in = [
        net.copy(gs.at[ypeer(d)], yr.at[d], yr.at[d], (r, ypeer(d) * 2 + c, h))
        for d in range(1, 8)
    ]
    lax.fori_loop(6, 8, head_step, 0)

    for m in y_in:
        m.wait_recv()
    piece = gs[y]
    for d in range(1, 8):
        piece = piece + yr[d]
    gyf[c, y] = piece
    yg_in = []
    for d in range(1, 8):
        src = (y + 8 - d) % 8
        yg_in.append(
            net.copy(gyf.at[c, y], gyf.at[c, y], gyf.at[c, src], (r, ypeer(d) * 2 + c, h))
        )
    c_first = net.copy(cy.at[1 - c], cfr, cfr, mate)

    k_all, v_all = acc[0] * scale, acc[1]
    kv_ref[0] = k_all[256:512].astype(BF16)
    kv_ref[1] = v_all[256:512].astype(BF16)
    ret[:, 0] = k_all[0:256].reshape(16, 16, 128).astype(BF16)
    ret[:, 1] = v_all[0:256].reshape(16, 16, 128).astype(BF16)

    for m in yg_in:
        m.wait_recv()
    last = net.copy(gyf.at[c], gyf.at[c], gyf.at[1 - c], mate)
    c_first.wait_recv()
    cgs[...] = (cy[c] + cfr[...]).reshape(8, 8, 256)
    c_in = [
        net.copy(cgs.at[ypeer(d)], cyr.at[d], cyr.at[d], (r, ypeer(d) * 2 + c, h))
        for d in range(1, 8)
    ]
    ret_arr = [
        net.copy(ret.at[fpeer(d)], ret_in.at[d], ret_in.at[d], (r, fpeer(d), h))
        for d in range(1, NF)
    ]
    last.wait_recv()

    low = gyf[0].reshape(192, 128)
    high = gyf[1].reshape(192, 128)
    fa[...] = low[0:128]
    li[1, 0:64], li[1, 64:128] = low[128:192], high[0:64]
    li[3] = high[64:192]
    whole_factor(fa, fx, li.at[0])
    i11 = li[0]
    l21 = exact(li[1], i11, 1, 1)
    fa[...] = li[3] - exact(l21, l21, 1, 1)
    li[2] = exact(l21, i11, 1, 0)

    for m in c_in:
        m.wait_recv()
    c_piece = cgs[y]
    for d in range(1, 8):
        c_piece = c_piece + cyr[d]
    cyf[c, y] = c_piece
    cg_in = []
    for d in range(1, NF):
        src = (f + NF - d) % NF
        cg_in.append(
            net.copy(cyf.at[c, y], cyf.at[c, y], cyf.at[src % 2, src // 2], (r, fpeer(d), h))
        )

    for m in ret_arr:
        m.wait_recv()
    ret_in[0] = ret[f]
    for s in range(16):
        tot = jnp.zeros((2, 16, 128), F32)
        for d in range(NF):
            tot = tot + jnp.where(slot_at(slots, f, d) == s, ret_in[d].astype(F32), 0.0)
        bys[s // 2, :, s % 2] = tot
    b_in = [
        net.copy(bys.at[zpeer(d)], bys_in.at[d], bys_in.at[d], (zpeer(d), f, h))
        for d in range(1, NR)
    ]

    whole_factor(fa, fx, li.at[1])
    i22 = li[1]
    i21 = -exact(i22, li[2], 1, 0)

    def times_inverse(m):
        first_part = exact(m[:, 0:128], i11, 1, 1)
        second = exact(m[:, 0:128], i21, 1, 1) + exact(m[:, 128:256], i22, 1, 1)
        return first_part, second

    for m in cg_in:
        m.wait_recv()
    b1, b2 = times_inverse(cyf[...].reshape(128, 256))
    back[:, 0:128] = b1
    back[:, 128:256] = b2
    bk = back[...]
    sq = jnp.sum(bk * bk, axis=0, keepdims=True)
    sqx[0] = sq
    x_in = [
        net.copy(sqx.at[0], sqx.at[d], sqx.at[d], (r, f, (h + d) % NH)) for d in range(1, NH)
    ]
    o1, o2 = times_inverse(pf[...].reshape(512, 256))
    orth[:, 0:128] = o1
    orth[:, 128:256] = o2
    for m in x_in:
        m.wait_recv()
    sqz[0] = (sqx[0] + sqx[2]) + (sqx[1] + sqx[3])
    q_in = [
        net.copy(sqz.at[0], sqz.at[d], sqz.at[d], (zpeer(d), f, h)) for d in range(1, NR)
    ]
    mo_ref[...] = total[...] - 0.05 * exact(orth[...], bk, 1, 1)
    for m in b_in:
        m.wait_recv()
    owned = bys[r]
    for d in range(1, NR):
        owned = owned + bys_in[d]
    pg_ref[...] = owned
    for m in q_in:
        m.wait_recv()
    squares = sqz[0]
    for d in range(1, NR):
        squares = squares + sqz[d]
    new = bk * lax.rsqrt(squares + 1e-06)
    bo_ref[...] = new
    upd_ref[...] = (GAIN * exact(orth[...], new, 1, 1)).astype(BF16)
    net.finish()


def slot_at(slots, f, d):
    at = (f + NF - d) % NF
    found = slots[0]
    for k in range(1, NF):
        found = jnp.where(at == k, slots[k], found)
    return found


def put(*refs):
    moves = [pltpu.make_async_copy(refs[k], refs[6 + k], refs[12].at[k]) for k in range(6)]
    for m in moves:
        m.start()
    for m in moves:
        m.wait()


def on_device(*args):
    vm = pl.BlockSpec(memory_space=pltpu.VMEM)
    hb = pl.BlockSpec(memory_space=pltpu.HBM)
    v = pltpu.VMEM
    outs = (
            jax.ShapeDtypeStruct((256, 1024), BF16),
            jax.ShapeDtypeStruct((2, 256, 128), BF16),
            jax.ShapeDtypeStruct((2, 2, 16, 128), F32),
            jax.ShapeDtypeStruct((512, 128), BF16),
            jax.ShapeDtypeStruct((512, 128), F32),
            jax.ShapeDtypeStruct((128, 256), F32),
    )
    s = pltpu.SMEM
    done = pl.pallas_call(
        kernel,
        out_shape=outs,
        in_specs=[hb] * 9 + [pl.BlockSpec(memory_space=pltpu.SMEM)] + [hb] * 3,
        out_specs=(vm,) * 6,
        scratch_shapes=[
            v((256, 1024), BF16), v((256, 128), BF16), v((256, 128), BF16), v((256, 1024), BF16),
            v((2, 16, 128), BF16), v((2, 16, 128), BF16), s((16,), jnp.int32),
            s((16,), jnp.int32), s((16,), jnp.int32), v((512, 128), BF16), v((512, 128), F32),
            v((128, 256), F32),
            v((512, 128), F32),
            v((8, 64, 256), F32),
            v((6, 64, 256), F32),
            v((2, 64, 256), F32),
            v((8, 16, 256), F32),
            v((8, 16, 256), F32),
            v((8, 64, 256), F32),
            v((2, 192, 128), F32),
            v((192, 128), F32),
            v((8, 24, 128), F32),
            v((8, 24, 128), F32),
            v((2, 8, 24, 128), F32),
            v((2, 64, 256), F32),
            v((64, 256), F32),
            v((8, 8, 256), F32),
            v((8, 8, 256), F32),
            v((2, 8, 8, 256), F32),
            v((8, 2, 16, 128), BF16),
            v((8, 2, 16, 128), BF16),
            v((16, 2, 16, 128), BF16),
            v((2, 32, 16, 128), BF16),
            v((512, 256), F32),
            v((256, 1024), BF16),
            v((128, 512), BF16),
            v((2, 512, 128), F32),
            v((16, 2, 16, 128), BF16),
            v((16, 2, 16, 128), BF16),
            v((8, 2, 2, 16, 128), F32),
            v((8, 2, 2, 16, 128), F32),
            v((4, 1, 256), F32),
            v((8, 1, 256), F32),
            v((128, 128), F32),
            v((128, 128), F32),
            v((4, 128, 128), F32),
            v((512, 256), F32),
            v((128, 256), F32),
            pltpu.SemaphoreType.DMA((12,)),
            pltpu.SemaphoreType.DMA((COPIES,)),
            pltpu.SemaphoreType.DMA((COPIES,)),
        ],
        compiler_params=pltpu.CompilerParams(
            collective_id=0, has_side_effects=True, vmem_limit_bytes=24 * 1024 * 1024
        ),
    )(*[a if k == 9 else pltpu.with_memory_space_constraint(a, pltpu.HBM) for k, a in enumerate(args)])
    return pl.pallas_call(
        put,
        out_shape=outs,
        in_specs=[vm] * 6,
        out_specs=(hb,) * 6,
        scratch_shapes=[pltpu.SemaphoreType.DMA((6,))],
        compiler_params=pltpu.CompilerParams(vmem_limit_bytes=24 * 1024 * 1024),
    )(*done)


def solution(mesh):
    placed = (
        P(("resp", "fsdp"), "head"),
        P(("resp", "fsdp"), "head"),
        P(("resp", "fsdp"), "head"),
        P(("resp", "fsdp"), "head"),
        P("resp", "fsdp", "head"),
        P("resp", "fsdp", "head"),
        P(),
        P(),
        P(),
        P(("resp", "fsdp")),
        P("fsdp", ("resp", "head")),
        P("fsdp", ("resp", "head")),
        P(("resp", "head"), None),
    )
    return jax.shard_map(
        on_device,
        mesh=mesh,
        in_specs=placed,
        out_specs=(
            P(("resp", "fsdp"), "head"),
            P(None, ("resp", "fsdp"), "head"),
            P(None, "resp", "fsdp", "head"),
            P("fsdp", ("resp", "head")),
            P("fsdp", ("resp", "head")),
            P(("resp", "head"), None),
        ),
        check_vma=False,
    )
```

```python
import functools
import math

import jax
import jax.numpy as jnp
from jax import lax
from jax.experimental import pallas as pl
from jax.experimental.pallas import tpu as pltpu
from jax.sharding import PartitionSpec as P

MESH = pl.DeviceIdType.MESH
HIGHEST = lax.Precision.HIGHEST
F32 = jnp.float32
BF16 = jnp.bfloat16

NR, NF, NH = 8, 16, 4
HD = 128
RANK = 256
GAIN = math.sqrt(8192 * 4096 / 256)
COPIES = 176


def mm(a, b, ca, cb, precision=None):
    return lax.dot_general(
        a, b, (((ca,), (cb,)), ((), ())), precision=precision, preferred_element_type=F32
    )


def exact(a, b, ca, cb):
    return mm(a, b, ca, cb, HIGHEST)


class Net:
    def __init__(self, sent, arrived):
        self.sent, self.arrived, self.n = sent, arrived, 0
        self.open = []

    def copy(self, src, dst, lands, device):
        at = self.n
        self.n += 1
        go = pltpu.make_async_remote_copy(
            src_ref=src, dst_ref=dst, send_sem=self.sent.at[at], recv_sem=self.arrived.at[at],
            device_id=device, device_id_type=MESH,
        )
        come = pltpu.make_async_remote_copy(
            src_ref=src, dst_ref=lands, send_sem=self.sent.at[at], recv_sem=self.arrived.at[at],
            device_id=device, device_id_type=MESH,
        )
        go.start()
        self.open.append(go)
        return come

    def finish(self):
        for c in self.open:
            c.wait_send()


def whole_factor(a_ref, x_ref, o_ref):
    row = lax.broadcasted_iota(jnp.int32, (8, 128), 0)
    r128 = lax.broadcasted_iota(jnp.int32, (128, 128), 0)
    c128 = lax.broadcasted_iota(jnp.int32, (128, 128), 1)
    x_ref[...] = jnp.where(r128 == c128, 1.0, 0.0).astype(F32)

    def line(v, j):
        return jnp.broadcast_to(v[j : j + 1, :], (8, 128))

    def lanes(v, start):
        return [
            jnp.take_along_axis(v, jnp.full((8, 128), start + j, jnp.int32), axis=1)
            for j in range(8)
        ]

    def reciprocal(v):
        guess = pl.reciprocal(v, approx=True)
        guess = guess * (2.0 - v * guess)
        return guess * (2.0 - v * guess)

    def root(v):
        guess = lax.rsqrt(v)
        return guess * (1.5 - 0.5 * v * guess * guess)

    def reduce_panel(z, zx, start):
        cols = lanes(z, start)
        spread = {(i, k): line(cols[k], i) for k in range(8) for i in range(k, 8)}
        out = jnp.zeros((8, 128), F32)
        for j in range(0, 8, 2):
            one, two = row == j, row == j + 1
            pair = one | two
            a, b, d = spread[j, j], spread[j + 1, j], spread[j + 1, j + 1]
            det = a * d - b * b
            inv = reciprocal(det)
            i11, i12, i22 = d * inv, -(b * inv), a * inv
            for i in range(j + 2, 8):
                e1 = spread[i, j] * i11 + spread[i, j + 1] * i12
                e2 = spread[i, j] * i12 + spread[i, j + 1] * i22
                for k in range(j + 2, i + 1):
                    spread[i, k] = spread[i, k] - (e1 * spread[k, j] + e2 * spread[k, j + 1])
            f1 = jnp.where(one, -i11, jnp.where(two, -i12, cols[j] * i11 + cols[j + 1] * i12))
            f2 = jnp.where(one, -i12, jnp.where(two, -i22, cols[j] * i12 + cols[j + 1] * i22))

            def sweep(v):
                return jnp.where(pair, 0.0, v) - (f1 * line(v, j) + f2 * line(v, j + 1))

            first, second = line(zx, j), line(zx, j + 1)
            up = reciprocal(a)
            out = jnp.where(one, first * root(a), out)
            out = jnp.where(two, (second - (b * up) * first) * root(det * up), out)
            for m in range(j + 2, 8):
                cols[m] = sweep(cols[m])
            z, zx = sweep(z), sweep(zx)
        return z, zx, out

    def take(v, c, lines):
        t = [c[j] * lines[j] for j in range(8)]
        return v - (((t[0] + t[1]) + (t[2] + t[3])) + ((t[4] + t[5]) + (t[6] + t[7])))

    z, zx, out = reduce_panel(a_ref[0:8, :], x_ref[0:8, :], 0)
    o_ref[0:8, :] = out

    def step(first, p, carry):
        z, zx = carry
        zs, zxs = [line(z, j) for j in range(8)], [line(zx, j) for j in range(8)]
        at = pl.ds(pl.multiple_of(p * 8 + 8, 8), 8)
        nz = a_ref[at, :]
        c = lanes(nz, p * 8)
        nz, nzx = take(nz, c, zs), take(x_ref[at, :], c, zxs)
        nz, nzx, out = reduce_panel(nz, nzx, p * 8 + 8)
        for t in range(first, 16):
            below = jnp.where(p + 1 < t, 1.0, 0.0).astype(F32)
            here = slice(8 * t, 8 * t + 8)
            a_t = a_ref[here, :]
            c = lanes(a_t * below, p * 8)
            a_ref[here, :] = take(a_t, c, zs)
            x_ref[here, :] = take(x_ref[here, :], c, zxs)
        o_ref[at, :] = out
        return nz, nzx

    carry = (z, zx)
    for low, high in ((0, 4), (4, 8), (8, 12), (12, 15)):
        carry = lax.fori_loop(low, high, functools.partial(step, low + 2), carry)


def kernel(
    q_hbm, sk_hbm, sv_hbm, do_hbm, pk_hbm, pv_hbm, counts_hbm, owner_hbm, pblk_hbm, rblk_ref,
    gq_hbm, mom_hbm, basis_hbm,
    dq_ref, kv_ref, pg_ref, upd_ref, mo_ref, bo_ref,
    q_ref, sk_ref, sv_ref, do_ref, pkv_ref, counts_ref, owner_ref, pblk_ref,
    gq_ref, mom_ref, basis_ref, total, pp, xr, xs, s1, zr, pf, gy, fr, gs, yr, gyf, cy, cfr, cgs, cyr, cyf, ev, sel, kvb, bias, gm, kt, acc,
    ret, ret_in, bys, bys_in, sqz, fa, fx, li, orth, back, loaded, sent, arrived,
):
    r, f, h = lax.axis_index("resp"), lax.axis_index("fsdp"), lax.axis_index("head")
    y, c = f // 2, f % 2
    net = Net(sent, arrived)
    right, left = (h + 1) % NH, (h + 3) % NH
    scale = HD ** -0.5

    def zpeer(d):
        return (r + d) % NR

    def fpeer(d):
        return (f + d) % NF

    def ypeer(d):
        return (y + d) % 8

    def load(k, src, dst):
        c = pltpu.make_async_copy(src, dst, loaded.at[k])
        c.start()
        return c

    mains = [
        load(0, mom_hbm, mom_ref), load(1, gq_hbm, gq_ref), load(2, basis_hbm, basis_ref),
    ]
    prompts = [
        load(3, pk_hbm, pkv_ref.at[0]), load(4, pv_hbm, pkv_ref.at[1]), load(5, counts_hbm, counts_ref),
        load(6, owner_hbm, owner_ref), load(7, pblk_hbm, pblk_ref),
    ]
    others = [
        load(8, do_hbm, do_ref), load(9, sk_hbm, sk_ref), load(10, sv_hbm, sv_ref),
        load(11, q_hbm, q_ref),
    ]

    barrier = pltpu.get_barrier_semaphore()
    for d in range(1, NR * NH):
        pl.semaphore_signal(
            barrier, inc=1, device_id=(zpeer(d // NH), f, (h + d) % NH), device_id_type=MESH
        )
    for d in range(1, NF):
        pl.semaphore_signal(barrier, inc=1, device_id=(r, fpeer(d), h), device_id_type=MESH)

    opp = (h + 2) % NH
    to_r, to_l = (r, f, right), (r, f, left)

    for m in mains:
        m.wait()
    total[...] = mom_ref[...] + gq_ref[...].astype(F32)

    def project(q):
        rows = total[pl.ds(pl.multiple_of(q * 128, 128), 128), :]
        pp[pl.ds(q * 8, 8)] = exact(rows, basis_ref[...], 1, 0).reshape(8, 16, 256)

    project(opp)
    pl.semaphore_wait(barrier, (NR * NH - 1) + (NF - 1))

    order = (2, 1, 3, 0)
    slot = [((r // 2 + e) % 4) * 2 for e in range(4)]
    rel_l, rel_r, dir_l, dir_r, com_l, com_r = {}, {}, {}, {}, {}, {}
    for e in order:
        rel_l[e] = net.copy(pp.at[opp * 8 + slot[e]], xr.at[0, e], xr.at[0, e], to_r)
        rel_r[e] = net.copy(pp.at[opp * 8 + slot[e] + 1], xr.at[1, e], xr.at[1, e], to_l)
    for m in prompts:
        m.wait()
    ev_in = []
    for d in range(1, NR):
        src = (r + NR - d) % NR
        ev_in.append(net.copy(pkv_ref, ev.at[r], ev.at[src], (zpeer(d), f, h)))
    project(right)
    project(left)
    for e in order:
        dir_l[e] = net.copy(pp.at[right * 8 + slot[e] + 1], xr.at[2, e], xr.at[2, e], to_r)
        dir_r[e] = net.copy(pp.at[left * 8 + slot[e]], xr.at[3, e], xr.at[3, e], to_l)
        rel_l[e].wait_recv()
        xs[0, e] = xr[0, e] + pp[right * 8 + slot[e]]
        com_l[e] = net.copy(xs.at[0, e], xr.at[4, e], xr.at[4, e], to_r)
        rel_r[e].wait_recv()
        xs[1, e] = xr[1, e] + pp[left * 8 + slot[e] + 1]
        com_r[e] = net.copy(xs.at[1, e], xr.at[5, e], xr.at[5, e], to_l)
    project(h)

    z_in = []
    ready = {2: (4,), 1: (2,), 3: (3, 5, 6), 0: (1, 7)}
    for e in order:
        for m in (dir_l, dir_r, com_l, com_r):
            m[e].wait_recv()
        even, odd = slot[e], slot[e] + 1
        s1[even] = pp[h * 8 + even] + (xr[3, e] + xr[4, e])
        s1[odd] = pp[h * 8 + odd] + (xr[2, e] + xr[5, e])
        for d in ready[e]:
            z_in.append(net.copy(s1.at[zpeer(d)], zr.at[d], zr.at[d], (zpeer(d), f, h)))

    ev[r] = pkv_ref[...]
    ends = []
    run = jnp.int32(0)
    for g in range(16):
        run = run + counts_ref[g]
        ends.append(run)

    def group_of(order):
        n = jnp.int32(0)
        for g in range(15):
            n = n + jnp.where(ends[g] <= order, 1, 0).astype(jnp.int32)
        return n

    slots = [owner_ref[group_of(r * NF + k)] for k in range(NF)]
    plen = pblk_ref[group_of(r * NF + f)] * 128
    rlen = rblk_ref[0] * 128
    for m in ev_in:
        m.wait_recv()
    for k in range(NF):
        sl = slots[k]
        sel[k, 0] = ev[sl // 2, 0, sl % 2]
        sel[k, 1] = ev[sl // 2, 1, sl % 2]
    kv_in = []
    for d in range(1, NF):
        src = (f + NF - d) % NF
        kv_in.append(net.copy(sel.at[fpeer(d)], kvb.at[:, f], kvb.at[:, src], (r, fpeer(d), h)))
    kvb[:, f] = sel[f]

    for m in others:
        m.wait()
    key = lax.broadcasted_iota(jnp.int32, (512, 256), 0)
    tok = lax.broadcasted_iota(jnp.int32, (512, 256), 1)
    inner = key - 256
    seen = ((key < 256) & (key < plen)) | ((key >= 256) & (inner <= tok) & (inner < rlen))
    bias[...] = jnp.where(seen, 0.0, -jnp.inf).astype(F32)
    live = lax.broadcasted_iota(jnp.int32, (256, 1024), 0) < rlen
    gm[...] = jnp.where(live, do_ref[...].astype(F32), 0.0).astype(BF16)
    kvb[0, 16:32] = sk_ref[...].reshape(16, 16, 128)
    kvb[1, 16:32] = sv_ref[...].reshape(16, 16, 128)
    acc[...] = jnp.zeros_like(acc)

    def head_step(k, carry):
        cols = pl.ds(pl.multiple_of(k * HD, HD), HD)
        q, g = q_ref[:, cols], gm[:, cols]
        s = mm(kvb[0].reshape(512, 128), q, 1, 1) * scale + bias[...]
        e = jnp.exp(s - jnp.max(s, axis=0, keepdims=True))
        p = (e * (1.0 / jnp.sum(e, axis=0, keepdims=True))).astype(BF16)
        dp = mm(kvb[1].reshape(512, 128), g, 1, 1)
        pw = p.astype(F32)
        ds = (pw * (dp - jnp.sum(pw * dp, axis=0, keepdims=True))).astype(BF16)
        dq_ref[:, cols] = (mm(kt[...], ds, 1, 0) * scale).T.astype(BF16)
        acc[0] += mm(ds, q, 1, 0)
        acc[1] += mm(p, g, 1, 0)
        return carry

    for m in z_in:
        m.wait_recv()
    mine = s1[r]
    for d in range(1, NR):
        mine = mine + zr[d]
    pf[h * 8 + r] = mine
    g_in = [None]
    for d in range(1, NR):
        src = (r + NR - d) % NR
        here = pf.at[h * 8 + r]
        g_in.append(net.copy(here, here, pf.at[h * 8 + src], (zpeer(d), f, h)))
    from_l, from_r, passed = {}, {}, []

    def spread(d):
        at = (r + NR - d) % NR
        here = pf.at[h * 8 + at]
        from_l[d] = net.copy(here, here, pf.at[left * 8 + at], to_r)
        from_r[d] = net.copy(here, here, pf.at[right * 8 + at], to_l)

    def relay(d):
        at = (r + NR - d) % NR
        if d % 2 == 0:
            from_l[d].wait_recv()
            here, there = pf.at[left * 8 + at], to_r
        else:
            from_r[d].wait_recv()
            here, there = pf.at[right * 8 + at], to_l
        passed.append(net.copy(here, here, pf.at[opp * 8 + at], there))

    spread(0)
    for m in kv_in:
        m.wait_recv()
    keys = kvb[0].reshape(512, 128)
    kt[...] = keys.astype(F32).T.astype(BF16)
    g_in[1].wait_recv()
    spread(1)
    g_in[7].wait_recv()
    spread(7)
    relay(0)
    lax.fori_loop(0, 1, head_step, 0)
    for one, two in ((2, 6), (3, 5)):
        g_in[one].wait_recv()
        spread(one)
        g_in[two].wait_recv()
        spread(two)
        if one == 2:
            relay(1)
            relay(7)
    g_in[4].wait_recv()
    spread(4)
    relay(2)
    relay(6)
    lax.fori_loop(1, 2, head_step, 0)
    relay(3)
    relay(5)
    relay(4)
    for d in range(NR):
        (from_r if d % 2 == 0 else from_l)[d].wait_recv()

    def gram_of(m):
        m1, m2 = m[:, 0:128], m[:, 128:256]
        return exact(m1, m1, 0, 0), exact(m2, m1, 0, 0), exact(m2, m2, 0, 0)

    def quarter(q):
        return pf[pl.ds(q * 8, 8)].reshape(128, 256)

    part = gram_of(jnp.concatenate([quarter(h), quarter(left), quarter(right)], 0))
    for m in passed:
        m.wait_recv()
    g11, g21, g22 = (a + b for a, b in zip(part, gram_of(quarter(opp))))
    gy[0, 0:128], gy[0, 128:192] = g11, g21[0:64]
    gy[1, 0:64], gy[1, 64:192] = g21[64:128], g22

    mate = (r, f + 1 - 2 * c, h)
    first = net.copy(gy.at[1 - c], fr, fr, mate)
    cross = exact(total[...], pf[...].reshape(512, 256), 0, 0)
    cy[0], cy[1] = cross[0:64], cross[64:128]
    first.wait_recv()
    gs[...] = (gy[c] + fr[...]).reshape(8, 24, 128)
    y_in = [
        net.copy(gs.at[ypeer(d)], yr.at[d], yr.at[d], (r, ypeer(d) * 2 + c, h))
        for d in range(1, 8)
    ]
    lax.fori_loop(2, 5, head_step, 0)

    for m in y_in:
        m.wait_recv()
    piece = gs[y]
    for d in range(1, 8):
        piece = piece + yr[d]
    gyf[c, y] = piece
    yg_in = []
    for d in range(1, 8):
        src = (y + 8 - d) % 8
        yg_in.append(
            net.copy(gyf.at[c, y], gyf.at[c, y], gyf.at[c, src], (r, ypeer(d) * 2 + c, h))
        )
    c_first = net.copy(cy.at[1 - c], cfr, cfr, mate)

    lax.fori_loop(5, 8, head_step, 0)
    k_all, v_all = acc[0] * scale, acc[1]
    kv_ref[0] = k_all[256:512].astype(BF16)
    kv_ref[1] = v_all[256:512].astype(BF16)
    ret[:, 0] = k_all[0:256].reshape(16, 16, 128).astype(BF16)
    ret[:, 1] = v_all[0:256].reshape(16, 16, 128).astype(BF16)

    for m in yg_in:
        m.wait_recv()
    last = net.copy(gyf.at[c], gyf.at[c], gyf.at[1 - c], mate)
    c_first.wait_recv()
    cgs[...] = (cy[c] + cfr[...]).reshape(8, 8, 256)
    c_in = [
        net.copy(cgs.at[ypeer(d)], cyr.at[d], cyr.at[d], (r, ypeer(d) * 2 + c, h))
        for d in range(1, 8)
    ]
    ret_arr = [
        net.copy(ret.at[fpeer(d)], ret_in.at[d], ret_in.at[d], (r, fpeer(d), h))
        for d in range(1, NF)
    ]
    last.wait_recv()

    low = gyf[0].reshape(192, 128)
    high = gyf[1].reshape(192, 128)
    fa[...] = low[0:128]
    li[1, 0:64], li[1, 64:128] = low[128:192], high[0:64]
    li[3] = high[64:192]
    whole_factor(fa, fx, li.at[0])
    i11 = li[0]
    l21 = exact(li[1], i11, 1, 1)
    fa[...] = li[3] - exact(l21, l21, 1, 1)
    li[2] = exact(l21, i11, 1, 0)

    for m in c_in:
        m.wait_recv()
    c_piece = cgs[y]
    for d in range(1, 8):
        c_piece = c_piece + cyr[d]
    cyf[c, y] = c_piece
    cg_in = []
    for d in range(1, NF):
        src = (f + NF - d) % NF
        cg_in.append(
            net.copy(cyf.at[c, y], cyf.at[c, y], cyf.at[src % 2, src // 2], (r, fpeer(d), h))
        )

    for m in ret_arr:
        m.wait_recv()
    ret_in[0] = ret[f]
    for s in range(16):
        tot = jnp.zeros((2, 16, 128), F32)
        for d in range(NF):
            tot = tot + jnp.where(slot_at(slots, f, d) == s, ret_in[d].astype(F32), 0.0)
        bys[s // 2, :, s % 2] = tot
    b_in = [
        net.copy(bys.at[zpeer(d)], bys_in.at[d], bys_in.at[d], (zpeer(d), f, h))
        for d in range(1, NR)
    ]

    whole_factor(fa, fx, li.at[1])
    i22 = li[1]
    i21 = -exact(i22, li[2], 1, 0)

    def times_inverse(m):
        first_part = exact(m[:, 0:128], i11, 1, 1)
        second = exact(m[:, 0:128], i21, 1, 1) + exact(m[:, 128:256], i22, 1, 1)
        return first_part, second

    for m in cg_in:
        m.wait_recv()
    b1, b2 = times_inverse(cyf[...].reshape(128, 256))
    back[:, 0:128] = b1
    back[:, 128:256] = b2
    bk = back[...]
    sq = jnp.sum(bk * bk, axis=0, keepdims=True)
    sqz[0] = sq
    q_in = []
    for d in range(1, NR * NH):
        peer = (zpeer(d // NH), f, (h + d) % NH)
        q_in.append(net.copy(sqz.at[0], sqz.at[d], sqz.at[d], peer))
    o1, o2 = times_inverse(pf[...].reshape(512, 256))
    orth[:, 0:128] = o1
    orth[:, 128:256] = o2
    mo_ref[...] = total[...] - 0.05 * exact(orth[...], bk, 1, 1)
    for m in b_in:
        m.wait_recv()
    owned = bys[r]
    for d in range(1, NR):
        owned = owned + bys_in[d]
    pg_ref[...] = owned
    net.finish()
    for m in q_in:
        m.wait_recv()
    squares = sqz[0]
    for d in range(1, NR * NH):
        squares = squares + sqz[d]
    new = bk * lax.rsqrt(squares + 1e-06)
    bo_ref[...] = new
    upd_ref[...] = (GAIN * exact(orth[...], new, 1, 1)).astype(BF16)
    assert net.n == COPIES


def slot_at(slots, f, d):
    at = (f + NF - d) % NF
    found = slots[0]
    for k in range(1, NF):
        found = jnp.where(at == k, slots[k], found)
    return found


def put(*refs):
    moves = [pltpu.make_async_copy(refs[k], refs[6 + k], refs[12].at[k]) for k in range(6)]
    for m in moves:
        m.start()
    for m in moves:
        m.wait()


def on_device(*args):
    vm = pl.BlockSpec(memory_space=pltpu.VMEM)
    hb = pl.BlockSpec(memory_space=pltpu.HBM)
    v = pltpu.VMEM
    outs = (
            jax.ShapeDtypeStruct((256, 1024), BF16),
            jax.ShapeDtypeStruct((2, 256, 128), BF16),
            jax.ShapeDtypeStruct((2, 2, 16, 128), F32),
            jax.ShapeDtypeStruct((512, 128), BF16),
            jax.ShapeDtypeStruct((512, 128), F32),
            jax.ShapeDtypeStruct((128, 256), F32),
    )
    s = pltpu.SMEM
    done = pl.pallas_call(
        kernel,
        out_shape=outs,
        in_specs=[hb] * 9 + [pl.BlockSpec(memory_space=pltpu.SMEM)] + [hb] * 3,
        out_specs=(vm,) * 6,
        scratch_shapes=[
            v((256, 1024), BF16), v((256, 128), BF16), v((256, 128), BF16), v((256, 1024), BF16),
            v((2, 2, 16, 128), BF16), s((16,), jnp.int32),
            s((16,), jnp.int32), s((16,), jnp.int32), v((512, 128), BF16), v((512, 128), F32),
            v((128, 256), F32),
            v((512, 128), F32),
            v((32, 16, 256), F32),
            v((6, 4, 16, 256), F32),
            v((2, 4, 16, 256), F32),
            v((8, 16, 256), F32),
            v((8, 16, 256), F32),
            v((32, 16, 256), F32),
            v((2, 192, 128), F32),
            v((192, 128), F32),
            v((8, 24, 128), F32),
            v((8, 24, 128), F32),
            v((2, 8, 24, 128), F32),
            v((2, 64, 256), F32),
            v((64, 256), F32),
            v((8, 8, 256), F32),
            v((8, 8, 256), F32),
            v((2, 8, 8, 256), F32),
            v((8, 2, 2, 16, 128), BF16),
            v((16, 2, 16, 128), BF16),
            v((2, 32, 16, 128), BF16),
            v((512, 256), F32),
            v((256, 1024), BF16),
            v((128, 512), BF16),
            v((2, 512, 128), F32),
            v((16, 2, 16, 128), BF16),
            v((16, 2, 16, 128), BF16),
            v((8, 2, 2, 16, 128), F32),
            v((8, 2, 2, 16, 128), F32),
            v((32, 1, 256), F32),
            v((128, 128), F32),
            v((128, 128), F32),
            v((4, 128, 128), F32),
            v((512, 256), F32),
            v((128, 256), F32),
            pltpu.SemaphoreType.DMA((12,)),
            pltpu.SemaphoreType.DMA((COPIES,)),
            pltpu.SemaphoreType.DMA((COPIES,)),
        ],
        compiler_params=pltpu.CompilerParams(
            collective_id=0, has_side_effects=True, vmem_limit_bytes=24 * 1024 * 1024
        ),
    )(*[a if k == 9 else pltpu.with_memory_space_constraint(a, pltpu.HBM) for k, a in enumerate(args)])
    return pl.pallas_call(
        put,
        out_shape=outs,
        in_specs=[vm] * 6,
        out_specs=(hb,) * 6,
        scratch_shapes=[pltpu.SemaphoreType.DMA((6,))],
        compiler_params=pltpu.CompilerParams(vmem_limit_bytes=24 * 1024 * 1024),
    )(*done)


def solution(mesh):
    placed = (
        P(("resp", "fsdp"), "head"),
        P(("resp", "fsdp"), "head"),
        P(("resp", "fsdp"), "head"),
        P(("resp", "fsdp"), "head"),
        P("resp", "fsdp", "head"),
        P("resp", "fsdp", "head"),
        P(),
        P(),
        P(),
        P(("resp", "fsdp")),
        P("fsdp", ("resp", "head")),
        P("fsdp", ("resp", "head")),
        P(("resp", "head"), None),
    )
    return jax.shard_map(
        on_device,
        mesh=mesh,
        in_specs=placed,
        out_specs=(
            P(("resp", "fsdp"), "head"),
            P(None, ("resp", "fsdp"), "head"),
            P(None, "resp", "fsdp", "head"),
            P("fsdp", ("resp", "head")),
            P("fsdp", ("resp", "head")),
            P(("resp", "head"), None),
        ),
        check_vma=False,
    )
```
